256 devices in a mesh: hid: 4 (over x_lo, core), tok: 64 (over x_hi, y, z).
Axes of the slice: x: 4 (x_hi: 2, x_lo: 2; x = x_hi * 2 + x_lo), y: 4, z: 8, core: 2. Of those that a mesh axis runs over, the one named last changes fastest.
Arguments:
- val_inputs: bfloat16 [256, 4096], P(None, 'tok'), may hold values from -6 to 6
- val_out_grad: bfloat16 [256, 4096], P(None, 'tok'), may hold values from -6 to 6
- w_gate: bfloat16 [4096, 14336], P('tok', 'hid'), may hold values from -0.09375 to 0.09375
- w_up: bfloat16 [4096, 14336], P('tok', 'hid'), may hold values from -0.09375 to 0.09375
- w_down: bfloat16 [14336, 4096], P('hid', 'tok'), may hold values from -0.046875 to 0.046875
- val_attn_inputs: bfloat16 [256, 4096], P('hid', 'tok'), may hold values from -6 to 6
- train_inputs: bfloat16 [163840, 4096], P(('hid', 'tok')), may hold values from -6 to 6
- train_grads: bfloat16 [163840, 4096], P(('hid', 'tok')), may hold values from -6 to 6
Outputs:
- influence: float32 [163840], P(('hid', 'tok'))
- val_grad: bfloat16 [256, 4096], P('hid', 'tok')
The draws below stay inside these ranges and needn't reach their ends.
All inputs are finite; a program needn't handle non-finite values.
Results may differ from the reference program's by a relative error of at most 0.0036.
Values may be sent and summed in bfloat16 or wider, within the bound.
No kernel may reach another device: no remote copies, remote signals or barrier semaphores. Data moves between devices by JAX's collectives and lax.ppermute only.
A program may use at most 128 MiB of HBM per device.

```python
import jax
import jax.numpy as jnp
from jax import lax

D = 4096
FF = 14336
VAL = 256
TRAIN_DEV = 640
TRAIN = 163840


def shard_levels(stream_key, dims, split, smallest, largest):
    loudness = 1.0
    for dim, parts in split:
        heights = jax.random.uniform(jax.random.fold_in(jax.random.fold_in(stream_key, 6), dim), (parts,), jnp.float32, smallest / len(split), largest / len(split))
        loudness = loudness * jnp.repeat(jnp.exp(heights), dims[dim] // parts).reshape((-1,) + (1,) * (len(dims) - 1 - dim))
    return loudness


def normal_values(rng, shape, scale, bound, split=(), kind=jnp.bfloat16):
    loudness = shard_levels(rng, shape, split, -0.22, 0.18) if split else 1.0
    drawn = jax.random.normal(rng, shape, jnp.float32) * scale * loudness
    return jnp.minimum(jnp.maximum(drawn, -bound), bound).astype(kind)


def setup_inputs(seed: int = 0) -> dict:
    key_of = jax.random.split(jax.random.key(seed), 9)
    val_inputs = normal_values(key_of[0], (VAL, D), 1.0, 6.0, ((1, 64),))
    val_out_grad = normal_values(key_of[1], (VAL, D), 1.0, 6.0, ((1, 64),))
    w_gate = normal_values(key_of[2], (D, FF), D ** -0.5, 0.09375, ((0, 64), (1, 4)))
    w_up = normal_values(key_of[3], (D, FF), D ** -0.5, 0.09375, ((0, 64), (1, 4)))
    w_down = normal_values(key_of[4], (FF, D), FF ** -0.5, 0.046875, ((0, 4), (1, 64)))
    val_attn_inputs = normal_values(key_of[5], (VAL, D), 1.0, 6.0, ((0, 4), (1, 64)))
    train_inputs = normal_values(key_of[6], (TRAIN, D), 1.0, 6.0, ((0, 256),))
    train_grads = normal_values(key_of[7], (TRAIN, D), 1.0, 6.0, ((0, 256),))
    return {"val_inputs": val_inputs, "val_out_grad": val_out_grad, "w_gate": w_gate, "w_up": w_up, "w_down": w_down, "val_attn_inputs": val_attn_inputs, "train_inputs": train_inputs, "train_grads": train_grads}


def reference(val_inputs, val_out_grad, w_gate, w_up, w_down, val_attn_inputs, train_inputs, train_grads):
    gate_pre = jnp.dot(val_inputs, w_gate, preferred_element_type=jnp.float32)
    up_pre = jnp.dot(val_inputs, w_up, preferred_element_type=jnp.float32)
    hid_grad = jnp.dot(val_out_grad, w_down.T, preferred_element_type=jnp.float32)
    logistic = jax.nn.sigmoid(gate_pre)
    grad_gate = (hid_grad * up_pre * logistic * (1.0 + gate_pre * (1.0 - logistic))).astype(jnp.bfloat16)
    grad_up = (hid_grad * gate_pre * logistic).astype(jnp.bfloat16)
    back_grad = jnp.dot(grad_gate, w_gate.T, preferred_element_type=jnp.float32) + jnp.dot(grad_up, w_up.T, preferred_element_type=jnp.float32)
    val_grad = (val_out_grad.astype(jnp.float32) + back_grad).astype(jnp.bfloat16)
    blocks = TRAIN // TRAIN_DEV
    train_in = train_inputs.reshape(blocks, TRAIN_DEV, D)
    train_gr = train_grads.reshape(blocks, TRAIN_DEV, D)

    def one_block(pair):
        in_gram = jnp.dot(pair[0], val_attn_inputs.T, preferred_element_type=jnp.float32)
        grad_gram = jnp.dot(pair[1], val_grad.T, preferred_element_type=jnp.float32)
        return lax.optimization_barrier(jnp.sum(in_gram * grad_gram, axis=1))
    totals = lax.map(one_block, (train_in, train_gr)).reshape(TRAIN)
    influence = totals / (D * jnp.sqrt(jnp.float32(VAL)))
    return (influence, val_grad)
```

```python
import math

import jax
import jax.numpy as jnp
from jax import lax
from jax.sharding import Mesh
from jax.sharding import PartitionSpec as P

PLANE = ("xh", "y")
CHIPS = ("xl", "xh", "y")
HIDPLANE = ("xl", "c", "xh", "y")
BF16 = jnp.bfloat16
F32 = jnp.float32


def trade(value, axes):
    return lax.all_to_all(value, axes, 0, 0, tiled=True)


def share(value, axes, count):
    return trade(jnp.broadcast_to(value[None], (count,) + value.shape), axes)


def dot_first(left, right):
    return lax.dot_general(left, right, (((0,), (0,)), ((), ())), preferred_element_type=F32)


def dot_last(left, right):
    return lax.dot_general(left, right, (((1,), (1,)), ((), ())), preferred_element_type=F32)


def act_grads(gate_pre, up_pre, hid_grad):
    logistic = jax.nn.sigmoid(gate_pre)
    grad_gate = (hid_grad * up_pre * logistic * (1.0 + gate_pre * (1.0 - logistic))).astype(BF16)
    grad_up = (hid_grad * gate_pre * logistic).astype(BF16)
    return jnp.concatenate([grad_gate, grad_up], axis=1)


def local(
    val_inputs, val_out_grad, w_gate, w_up, w_down, val_attn_inputs, train_inputs, train_grads
):
    feats, units = w_gate.shape
    vals = val_inputs.shape[0]
    n_plane = lax.axis_size(PLANE)
    n_z = lax.axis_size("z")
    n_chips = lax.axis_size(CHIPS)
    n_hidplane = lax.axis_size(HIDPLANE)
    own = units // n_plane
    wide = feats * n_plane

    def spread(weight):
        return weight.reshape(feats, n_plane, own)

    def same(value):
        return jnp.broadcast_to(value[:, None], (feats, n_plane, vals))

    sent = jnp.concatenate(
        [
            spread(w_gate),
            spread(w_up),
            spread(w_down.T),
            same(val_inputs.T),
            same(val_out_grad.T),
        ],
        axis=2,
    ).transpose(1, 0, 2)
    got = trade(sent, PLANE).reshape(wide, 3 * own + 2 * vals)
    gate_w, up_w, down_w = got[:, :own], got[:, own : 2 * own], got[:, 2 * own : 3 * own]
    inputs_t, out_grad_t = got[:, 3 * own : 3 * own + vals], got[:, 3 * own + vals :]
    partial = jnp.concatenate(
        [dot_first(inputs_t, got[:, : 2 * own]), dot_first(out_grad_t, down_w)], axis=1
    ).astype(BF16)
    rows_z = vals // n_z
    pre = jnp.sum(trade(partial.reshape(n_z, rows_z, 3 * own), "z").astype(F32), axis=0)
    grads = act_grads(pre[:, :own], pre[:, own : 2 * own], pre[:, 2 * own :])
    attn_rows = val_attn_inputs.shape[0]
    attn_wide = attn_rows * feats // rows_z
    back = share(
        jnp.concatenate([grads, val_attn_inputs.reshape(rows_z, attn_wide)], axis=1), "z", n_z
    )
    grads = back[:, :, : 2 * own].reshape(vals, 2 * own)
    attn = back[:, :, 2 * own :].reshape(n_z, attn_rows, feats)
    part = dot_last(grads[:, :own], gate_w) + dot_last(grads[:, own:], up_w)
    chunk = vals // n_hidplane
    dx = jnp.sum(trade(part.reshape(n_hidplane, chunk, wide), HIDPLANE), axis=0)
    row = lax.axis_index(HIDPLANE) * chunk
    mine = lax.dynamic_slice_in_dim(out_grad_t, row, chunk, 1).T
    val_grad = (mine.astype(F32) + dx).astype(BF16)
    width = train_inputs.shape[1]
    val_z = share(val_grad, "z", n_z).reshape(n_z, chunk, n_plane, feats)
    val_z = val_z.transpose(1, 2, 0, 3).reshape(chunk, width)
    attn_z = attn.transpose(1, 0, 2).reshape(attn_rows // chunk, chunk, n_z * feats)
    attn_z = attn_z.transpose(1, 0, 2).reshape(chunk, attn_rows * feats * n_z // chunk)
    both = share(jnp.concatenate([val_z, attn_z], axis=1), CHIPS, n_chips)
    swap = [(0, 1), (1, 0)]
    other = lax.ppermute(both, "c", swap)
    xl_size = n_chips // n_plane

    def rows_of(block):
        val_rows = block[:, :, :width].reshape(n_chips * chunk, width)
        att = block[:, :, width:].reshape(xl_size, n_plane, chunk, attn_rows // chunk, n_z * feats)
        att = att.transpose(0, 3, 2, 1, 4).reshape(xl_size * attn_rows, width)
        return val_rows, att

    val_a, att_a = rows_of(both)
    val_b, att_b = rows_of(other)
    val_all = jnp.concatenate([val_a, val_b], axis=0)
    att_all = jnp.concatenate([att_a, att_b], axis=0)
    total = jnp.sum(dot_last(train_inputs, att_all) * dot_last(train_grads, val_all), axis=1)
    influence = total / (width * math.sqrt(vals))
    block = lax.dynamic_slice(
        val_a,
        (lax.axis_index("xl") * attn_rows, lax.axis_index(("xh", "y", "z")) * feats),
        (attn_rows, feats),
    )
    return (influence, block)


def solution(mesh):
    fine = Mesh(mesh.devices.reshape(2, 2, 2, 4, 8), ("xl", "c", "xh", "y", "z"))
    tok = ("xh", "y", "z")
    hid = ("xl", "c")
    placed = (
        P(None, tok),
        P(None, tok),
        P(tok, hid),
        P(tok, hid),
        P(hid, tok),
        P(hid, tok),
        P(hid + tok, None),
        P(hid + tok, None),
    )
    return jax.shard_map(
        local,
        mesh=fine,
        in_specs=placed,
        out_specs=(P(hid + tok), P(hid, tok)),
        check_vma=False,
    )
```

```python
import math

import jax
import jax.numpy as jnp
from jax import lax
from jax.sharding import Mesh
from jax.sharding import PartitionSpec as P


PLANE = ("xh", "y")
CHIPS = ("xl", "xh", "y")
HIDPLANE = ("xl", "c", "xh", "y")
BF16 = jnp.bfloat16
F32 = jnp.float32


MOVES = (
    ("z", 8, 1, 1),
    ("z", 8, 2, 1),
    ("z", 8, 4, 1),
    ("y", 4, 1, 1),
    ("y", 4, 2, 1),
    ("xh", 2, 1, 1),
    ("xl", 2, 1, 0),
)


def trade(value, axes):
    return lax.all_to_all(value, axes, 0, 0, tiled=True)


def share(value, axes, count):
    return trade(jnp.broadcast_to(value[None], (count,) + value.shape), axes)


def dot_first(left, right):
    return lax.dot_general(left, right, (((0,), (0,)), ((), ())), preferred_element_type=F32)


def dot_last(left, right):
    return lax.dot_general(left, right, (((1,), (1,)), ((), ())), preferred_element_type=F32)


def act_grads(gate_pre, up_pre, hid_grad):
    logistic = jax.nn.sigmoid(gate_pre)
    grad_gate = (hid_grad * up_pre * logistic * (1.0 + gate_pre * (1.0 - logistic))).astype(BF16)
    grad_up = (hid_grad * gate_pre * logistic).astype(BF16)
    return jnp.concatenate([grad_gate, grad_up], axis=1)


def local(
    val_inputs, val_out_grad, w_gate, w_up, w_down, val_attn_inputs, train_inputs, train_grads
):
    feats, units = w_gate.shape
    vals = val_inputs.shape[0]
    n_plane = lax.axis_size(PLANE)
    n_z = lax.axis_size("z")
    n_chips = lax.axis_size(CHIPS)
    n_hidplane = lax.axis_size(HIDPLANE)
    own = units // n_plane
    wide = feats * n_plane

    width = train_inputs.shape[1]
    attn_rows = val_attn_inputs.shape[0]
    chunk = vals // n_hidplane
    rows_z = vals // n_z
    swap = [(0, 1), (1, 0)]
    first_w, first_down = 2 * vals, 2 * vals + 2 * own

    def spread(weight):
        return weight.reshape(feats, n_plane, own)

    def same(value):
        return jnp.broadcast_to(value[:, None], (feats, n_plane, vals))

    row = lax.axis_index(HIDPLANE) * chunk
    attn = val_attn_inputs
    for axis, count, bit, dim in MOVES:
        pairs = [(i, i ^ bit) for i in range(count)]
        theirs = lax.ppermute(attn, axis, pairs)
        high = (lax.axis_index(axis) & bit) != 0
        attn = jnp.concatenate(
            [jnp.where(high, theirs, attn), jnp.where(high, attn, theirs)], axis=dim
        )
    sent = jnp.concatenate(
        [same(val_inputs.T), same(val_out_grad.T), spread(w_gate), spread(w_up), spread(w_down.T)],
        axis=2,
    ).transpose(1, 0, 2)
    got = trade(sent, PLANE).reshape(wide, 3 * own + 2 * vals)
    back_w = got[:, first_w:first_down]
    partial = jnp.concatenate(
        [dot_first(got[:, :vals], back_w), dot_first(got[:, vals:first_w], got[:, first_down:])],
        axis=1,
    ).astype(BF16)
    parts = trade(partial.reshape(n_z, rows_z, 3 * own), "z")
    pre = jnp.sum(parts.astype(F32), axis=0)
    grads = act_grads(pre[:, :own], pre[:, own : 2 * own], pre[:, 2 * own :])
    grads = share(grads, "z", n_z).reshape(vals, 2 * own)
    attn_other = lax.ppermute(attn, "c", swap)
    part = dot_last(grads, back_w)
    parts = trade(part.reshape(n_hidplane, chunk, wide), HIDPLANE)

    gram_own = lax.optimization_barrier(dot_last(train_inputs, attn))
    gram_other = lax.optimization_barrier(dot_last(train_inputs, attn_other))
    dx = jnp.sum(parts, axis=0)
    mine = lax.dynamic_slice_in_dim(got[:, vals:first_w], row, chunk, 1).T
    val_grad = (mine.astype(F32) + dx).astype(BF16)
    val_z = share(val_grad, "z", n_z).reshape(n_z, chunk, n_plane, feats)
    val_z = val_z.transpose(1, 2, 0, 3).reshape(chunk, width)
    val_own = share(val_z, CHIPS, n_chips).reshape(n_chips * chunk, width)
    val_other = lax.ppermute(val_own, "c", swap)
    total = jnp.sum(gram_own * dot_last(train_grads, val_own), axis=1)
    total = total + jnp.sum(gram_other * dot_last(train_grads, val_other), axis=1)
    influence = total / (width * math.sqrt(vals))
    block = lax.dynamic_slice(val_own, (lax.axis_index("xl") * attn_rows, lax.axis_index(("xh", "y", "z")) * feats), (attn_rows, feats))
    return (influence, block)


def solution(mesh):
    fine = Mesh(mesh.devices.reshape(2, 2, 2, 4, 8), ("xl", "c", "xh", "y", "z"))
    tok = ("xh", "y", "z")
    hid = ("xl", "c")
    placed = (
        P(None, tok),
        P(None, tok),
        P(tok, hid),
        P(tok, hid),
        P(hid, tok),
        P(hid, tok),
        P(hid + tok, None),
        P(hid + tok, None),
    )
    return jax.shard_map(
        local,
        mesh=fine,
        in_specs=placed,
        out_specs=(P(hid + tok), P(hid, tok)),
        check_vma=False,
    )
```

```python
import functools
import math

import jax
import jax.numpy as jnp
from jax import lax
from jax.experimental import pallas as pl
from jax.experimental.pallas import tpu as pltpu
from jax.sharding import Mesh
from jax.sharding import PartitionSpec as P


PLANE = ("xh", "y")
CHIPS = ("xl", "xh", "y")
HIDPLANE = ("xl", "c", "xh", "y")
BF16 = jnp.bfloat16
F32 = jnp.float32


MOVES = (
    ("z", 8, 1, 1),
    ("z", 8, 2, 1),
    ("z", 8, 4, 1),
    ("y", 4, 1, 1),
    ("y", 4, 2, 1),
    ("xh", 2, 1, 1),
    ("xl", 2, 1, 0),
)


def trade(value, axes):
    return lax.all_to_all(value, axes, 0, 0, tiled=True)


def share(value, axes, count):
    return trade(jnp.broadcast_to(value[None], (count,) + value.shape), axes)


def dot_first(left, right):
    return lax.dot_general(left, right, (((0,), (0,)), ((), ())), preferred_element_type=F32)


def dot_last(left, right):
    return lax.dot_general(left, right, (((1,), (1,)), ((), ())), preferred_element_type=F32)


def pack_kernel(in_ref, grad_ref, gate_ref, up_ref, down_ref, out_ref, held, sems):
    vals = in_ref.shape[1]
    own = (out_ref.shape[2] - 2 * vals) // 3
    copies = []
    for peer in range(out_ref.shape[0]):
        here = slice(peer * own, (peer + 1) * own)
        held[peer, :, :vals] = in_ref[...]
        held[peer, :, vals : 2 * vals] = grad_ref[...]
        start = 2 * vals
        for ref in (gate_ref, up_ref, down_ref):
            held[peer, :, start : start + own] = ref[:, here]
            start += own
        copies.append(pltpu.make_async_copy(held.at[peer], out_ref.at[peer], sems.at[peer]))
        copies[-1].start()
    for copy in copies:
        copy.wait()


def pack(inputs_t, out_grad_t, w_gate, w_up, w_down_t, peers):
    feats, vals = inputs_t.shape
    shape = (peers, feats, 2 * vals + 3 * (w_gate.shape[1] // peers))
    return pl.pallas_call(
        pack_kernel,
        out_specs=pl.BlockSpec(memory_space=pl.ANY),
        out_shape=jax.ShapeDtypeStruct(shape, BF16),
        scratch_shapes=[pltpu.VMEM(shape, BF16), pltpu.SemaphoreType.DMA((peers,))],
        name="pack",
    )(inputs_t, out_grad_t, w_gate, w_up, w_down_t)


def gram_kernel(train_ref, val_ref, out_ref):
    out_ref[...] = dot_last(val_ref[...], train_ref[...])


def gram(train, val):
    tokens, width = train.shape
    rows = val.shape[0]
    block = 128
    return pl.pallas_call(
        gram_kernel,
        grid=(tokens // block,),
        in_specs=[
            pl.BlockSpec((block, width), lambda i: (i, 0)),
            pl.BlockSpec((rows, width), lambda i: (0, 0)),
        ],
        out_specs=pl.BlockSpec((rows, block), lambda i: (0, i)),
        out_shape=jax.ShapeDtypeStruct((rows, tokens), F32),
        compiler_params=pltpu.CompilerParams(vmem_limit_bytes=10 * 1024 * 1024),
        name="gram",
    )(train, val)


def pair_kernel(scale, train_ref, own_ref, other_ref, gram_own_ref, gram_other_ref, out_ref, block_ref):
    rows, feats = block_ref.shape
    tile = (lax.axis_index("xh") * 4 + lax.axis_index("y")) * 8 + lax.axis_index("z")
    row = pl.multiple_of(lax.axis_index("xl") * rows, rows)
    col = pl.multiple_of((tile // 2) * (2 * feats), 2 * feats)
    found = own_ref[pl.ds(row, rows), pl.ds(col, 2 * feats)].astype(F32)
    half = jnp.where(tile % 2 == 0, found[:, :feats], found[:, feats:])
    block_ref[...] = half.astype(BF16)
    val = jnp.concatenate([own_ref[...], other_ref[...]], axis=0)
    grad_gram = dot_last(val, train_ref[...])
    count = own_ref.shape[0]
    total = gram_own_ref[...] * grad_gram[:count] + gram_other_ref[...] * grad_gram[count:]
    total = jnp.sum(total, axis=0, keepdims=True) * scale
    out_ref[...] = total.reshape(out_ref.shape)


def pair_values(scale, train, own, other, gram_own, gram_other, rows, feats):
    vmem = pl.BlockSpec(memory_space=pltpu.VMEM)
    return pl.pallas_call(
        functools.partial(pair_kernel, scale),
        out_shape=(
            jax.ShapeDtypeStruct((train.shape[0],), F32),
            jax.ShapeDtypeStruct((rows, feats), BF16),
        ),
        in_specs=[vmem] * 5,
        out_specs=(vmem, vmem),
        compiler_params=pltpu.CompilerParams(vmem_limit_bytes=24 * 1024 * 1024),
        name="pair_values",
    )(train, own, other, gram_own, gram_other)


def act_grads(gate_pre, up_pre, hid_grad):
    logistic = jax.nn.sigmoid(gate_pre)
    grad_gate = (hid_grad * up_pre * logistic * (1.0 + gate_pre * (1.0 - logistic))).astype(BF16)
    grad_up = (hid_grad * gate_pre * logistic).astype(BF16)
    return jnp.concatenate([grad_gate, grad_up], axis=1)


def local(
    val_inputs, val_out_grad, w_gate, w_up, w_down, val_attn_inputs, train_inputs, train_grads
):
    feats, units = w_gate.shape
    vals = val_inputs.shape[0]
    n_plane = lax.axis_size(PLANE)
    n_z = lax.axis_size("z")
    n_chips = lax.axis_size(CHIPS)
    n_hidplane = lax.axis_size(HIDPLANE)
    own = units // n_plane
    wide = feats * n_plane

    width = train_inputs.shape[1]
    attn_rows = val_attn_inputs.shape[0]
    chunk = vals // n_hidplane
    rows_z = vals // n_z
    swap = [(0, 1), (1, 0)]
    first_w, first_down = 2 * vals, 2 * vals + 2 * own

    row = lax.axis_index(HIDPLANE) * chunk
    attn = val_attn_inputs
    for axis, count, bit, dim in MOVES:
        pairs = [(i, i ^ bit) for i in range(count)]
        theirs = lax.ppermute(attn, axis, pairs)
        high = (lax.axis_index(axis) & bit) != 0
        attn = jnp.concatenate(
            [jnp.where(high, theirs, attn), jnp.where(high, attn, theirs)], axis=dim
        )
    sent = pack(val_inputs.T, val_out_grad.T, w_gate, w_up, w_down.T, n_plane)
    got = trade(sent, PLANE).reshape(wide, 3 * own + 2 * vals)
    back_w = got[:, first_w:first_down]
    partial = jnp.concatenate(
        [dot_first(got[:, :vals], back_w), dot_first(got[:, vals:first_w], got[:, first_down:])],
        axis=1,
    ).astype(BF16)
    parts = trade(partial.reshape(n_z, rows_z, 3 * own), "z")
    pre = jnp.sum(parts.astype(F32), axis=0)
    grads = act_grads(pre[:, :own], pre[:, own : 2 * own], pre[:, 2 * own :])
    grads = share(grads, "z", n_z).reshape(vals, 2 * own)
    attn_other = lax.ppermute(attn, "c", swap)
    part = dot_last(grads, back_w)
    parts = trade(part.reshape(n_hidplane, chunk, wide), HIDPLANE)

    gram_own = gram(train_inputs, attn)
    gram_other = gram(train_inputs, attn_other)
    dx = jnp.sum(parts, axis=0)
    mine = lax.dynamic_slice_in_dim(got[:, vals:first_w], row, chunk, 1).T
    mine = lax.optimization_barrier(mine)
    val_grad = (mine.astype(F32) + dx).astype(BF16)
    val_z = share(val_grad, "z", n_z).reshape(n_z, chunk, n_plane, feats)
    val_z = val_z.transpose(1, 2, 0, 3).reshape(chunk, width)
    val_own = share(val_z, CHIPS, n_chips).reshape(n_chips * chunk, width)
    val_other = lax.ppermute(val_own, "c", swap)
    scale = 1.0 / (width * math.sqrt(vals))
    influence, block = pair_values(
        scale, train_grads, val_own, val_other, gram_own, gram_other, attn_rows, feats
    )
    return (influence, block)


def solution(mesh):
    fine = Mesh(mesh.devices.reshape(2, 2, 2, 4, 8), ("xl", "c", "xh", "y", "z"))
    tok = ("xh", "y", "z")
    hid = ("xl", "c")
    placed = (
        P(None, tok),
        P(None, tok),
        P(tok, hid),
        P(tok, hid),
        P(hid, tok),
        P(hid, tok),
        P(hid + tok, None),
        P(hid + tok, None),
    )
    return jax.shard_map(
        local,
        mesh=fine,
        in_specs=placed,
        out_specs=(P(hid + tok), P(hid, tok)),
        check_vma=False,
    )
```

```python
import functools
import math

import jax
import jax.numpy as jnp
from jax import lax
from jax.experimental import pallas as pl
from jax.experimental.pallas import tpu as pltpu
from jax.sharding import Mesh
from jax.sharding import PartitionSpec as P


PLANE = ("xh", "y")
CHIPS = ("xl", "xh", "y")
HIDPLANE = ("xl", "c", "xh", "y")
BF16 = jnp.bfloat16
F32 = jnp.float32


MOVES = (
    ("z", 8, 1, 1),
    ("z", 8, 2, 1),
    ("z", 8, 4, 1),
    ("y", 4, 1, 1),
    ("y", 4, 2, 1),
    ("xh", 2, 1, 1),
    ("xl", 2, 1, 0),
)


def trade(value, axes):
    return lax.all_to_all(value, axes, 0, 0, tiled=True)


def share(value, axes, count):
    return trade(jnp.broadcast_to(value[None], (count,) + value.shape), axes)


def dot_first(left, right):
    return lax.dot_general(left, right, (((0,), (0,)), ((), ())), preferred_element_type=F32)


def dot_last(left, right):
    return lax.dot_general(left, right, (((1,), (1,)), ((), ())), preferred_element_type=F32)


def pack_kernel(in_ref, grad_ref, gate_ref, up_ref, down_ref, out_ref, held, sems):
    vals = in_ref.shape[1]
    own = (out_ref.shape[2] - 2 * vals) // 3
    copies = []
    for peer in range(out_ref.shape[0]):
        here = slice(peer * own, (peer + 1) * own)
        held[peer, :, :vals] = in_ref[...]
        held[peer, :, vals : 2 * vals] = grad_ref[...]
        start = 2 * vals
        for ref in (gate_ref, up_ref, down_ref):
            held[peer, :, start : start + own] = ref[:, here]
            start += own
        copies.append(pltpu.make_async_copy(held.at[peer], out_ref.at[peer], sems.at[peer]))
        copies[-1].start()
    for copy in copies:
        copy.wait()


def pack(inputs_t, out_grad_t, w_gate, w_up, w_down_t, peers):
    feats, vals = inputs_t.shape
    shape = (peers, feats, 2 * vals + 3 * (w_gate.shape[1] // peers))
    return pl.pallas_call(
        pack_kernel,
        out_specs=pl.BlockSpec(memory_space=pl.ANY),
        out_shape=jax.ShapeDtypeStruct(shape, BF16),
        scratch_shapes=[pltpu.VMEM(shape, BF16), pltpu.SemaphoreType.DMA((peers,))],
        name="pack",
    )(inputs_t, out_grad_t, w_gate, w_up, w_down_t)


def gram_kernel(train_ref, val_ref, out_ref):
    out_ref[...] = dot_last(val_ref[...], train_ref[...])


def gram(train, val):
    tokens, width = train.shape
    rows = val.shape[0]
    block = 128
    return pl.pallas_call(
        gram_kernel,
        grid=(tokens // block,),
        in_specs=[
            pl.BlockSpec((block, width), lambda i: (i, 0)),
            pl.BlockSpec((rows, width), lambda i: (0, 0)),
        ],
        out_specs=pl.BlockSpec((rows, block), lambda i: (0, i)),
        out_shape=jax.ShapeDtypeStruct((rows, tokens), F32),
        compiler_params=pltpu.CompilerParams(vmem_limit_bytes=10 * 1024 * 1024),
        name="gram",
    )(train, val)


def block_kernel(own_ref, block_ref):
    rows, feats = block_ref.shape
    tile = (lax.axis_index("xh") * 4 + lax.axis_index("y")) * 8 + lax.axis_index("z")
    row = pl.multiple_of(lax.axis_index("xl") * rows, rows)
    col = pl.multiple_of((tile // 2) * (2 * feats), 2 * feats)
    found = own_ref[pl.ds(row, rows), pl.ds(col, 2 * feats)].astype(F32)
    half = jnp.where(tile % 2 == 0, found[:, :feats], found[:, feats:])
    block_ref[...] = half.astype(BF16)


def pair_kernel(scale, train_ref, own_ref, other_ref, gram_own_ref, gram_other_ref, out_ref):
    val = jnp.concatenate([own_ref[...], other_ref[...]], axis=0)
    grad_gram = dot_last(val, train_ref[...])
    count = own_ref.shape[0]
    total = gram_own_ref[...] * grad_gram[:count] + gram_other_ref[...] * grad_gram[count:]
    total = jnp.sum(total, axis=0, keepdims=True) * scale
    out_ref[...] = total.reshape(out_ref.shape)


VMEM = pl.BlockSpec(memory_space=pltpu.VMEM)
COVER = pl.CostEstimate(flops=10**10, bytes_accessed=32 * 2**20, transcendentals=0)


def own_block(own, rows, feats):
    return pl.pallas_call(
        block_kernel,
        out_shape=jax.ShapeDtypeStruct((rows, feats), BF16),
        in_specs=[VMEM],
        out_specs=VMEM,
        compiler_params=pltpu.CompilerParams(vmem_limit_bytes=8 * 1024 * 1024),
        cost_estimate=COVER,
        name="own_block",
    )(own)


def pair_values(scale, train, own, other, gram_own, gram_other):
    return pl.pallas_call(
        functools.partial(pair_kernel, scale),
        out_shape=jax.ShapeDtypeStruct((train.shape[0],), F32),
        in_specs=[VMEM] * 5,
        out_specs=VMEM,
        compiler_params=pltpu.CompilerParams(vmem_limit_bytes=24 * 1024 * 1024),
        name="pair_values",
    )(train, own, other, gram_own, gram_other)


def act_grads(gate_pre, up_pre, hid_grad):
    logistic = jax.nn.sigmoid(gate_pre)
    grad_gate = (hid_grad * up_pre * logistic * (1.0 + gate_pre * (1.0 - logistic))).astype(BF16)
    grad_up = (hid_grad * gate_pre * logistic).astype(BF16)
    return jnp.concatenate([grad_gate, grad_up], axis=1)


def local(
    val_inputs, val_out_grad, w_gate, w_up, w_down, val_attn_inputs, train_inputs, train_grads
):
    feats, units = w_gate.shape
    vals = val_inputs.shape[0]
    n_plane = lax.axis_size(PLANE)
    n_z = lax.axis_size("z")
    n_chips = lax.axis_size(CHIPS)
    n_hidplane = lax.axis_size(HIDPLANE)
    own = units // n_plane
    wide = feats * n_plane

    width = train_inputs.shape[1]
    attn_rows = val_attn_inputs.shape[0]
    chunk = vals // n_hidplane
    rows_z = vals // n_z
    swap = [(0, 1), (1, 0)]
    first_w, first_down = 2 * vals, 2 * vals + 2 * own

    row = lax.axis_index(HIDPLANE) * chunk
    attn = val_attn_inputs
    for axis, count, bit, dim in MOVES:
        pairs = [(i, i ^ bit) for i in range(count)]
        theirs = lax.ppermute(attn, axis, pairs)
        high = (lax.axis_index(axis) & bit) != 0
        attn = jnp.concatenate(
            [jnp.where(high, theirs, attn), jnp.where(high, attn, theirs)], axis=dim
        )
    sent = pack(val_inputs.T, val_out_grad.T, w_gate, w_up, w_down.T, n_plane)
    got = trade(sent, PLANE).reshape(wide, 3 * own + 2 * vals)
    back_w = got[:, first_w:first_down]
    partial = jnp.concatenate(
        [dot_first(got[:, :vals], back_w), dot_first(got[:, vals:first_w], got[:, first_down:])],
        axis=1,
    ).astype(BF16)
    parts = trade(partial.reshape(n_z, rows_z, 3 * own), "z")
    pre = jnp.sum(parts.astype(F32), axis=0)
    grads = act_grads(pre[:, :own], pre[:, own : 2 * own], pre[:, 2 * own :])
    grads = share(grads, "z", n_z).reshape(vals, 2 * own)
    attn_other = lax.ppermute(attn, "c", swap)
    part = dot_last(grads, back_w)
    parts = trade(part.reshape(n_hidplane, chunk, wide), HIDPLANE)

    gram_own = gram(train_inputs, attn)
    gram_other = gram(train_inputs, attn_other)
    dx = jnp.sum(parts, axis=0)
    mine = lax.dynamic_slice_in_dim(got[:, vals:first_w], row, chunk, 1).T
    mine = lax.optimization_barrier(mine)
    val_grad = (mine.astype(F32) + dx).astype(BF16)
    val_z = share(val_grad, "z", n_z).reshape(n_z, chunk, n_plane, feats)
    val_z = val_z.transpose(1, 2, 0, 3).reshape(chunk, width)
    val_own = share(val_z, CHIPS, n_chips).reshape(n_chips * chunk, width)
    val_other = lax.ppermute(val_own, "c", swap)
    block = own_block(val_own, attn_rows, feats)
    scale = 1.0 / (width * math.sqrt(vals))
    influence = pair_values(scale, train_grads, val_own, val_other, gram_own, gram_other)
    return (influence, block)


def solution(mesh):
    fine = Mesh(mesh.devices.reshape(2, 2, 2, 4, 8), ("xl", "c", "xh", "y", "z"))
    tok = ("xh", "y", "z")
    hid = ("xl", "c")
    placed = (
        P(None, tok),
        P(None, tok),
        P(tok, hid),
        P(tok, hid),
        P(hid, tok),
        P(hid, tok),
        P(hid + tok, None),
        P(hid + tok, None),
    )
    return jax.shard_map(
        local,
        mesh=fine,
        in_specs=placed,
        out_specs=(P(hid + tok), P(hid, tok)),
        check_vma=False,
    )
```

```python
import functools
import math

import jax
import jax.numpy as jnp
from jax import lax
from jax.experimental import pallas as pl
from jax.experimental.pallas import tpu as pltpu
from jax.sharding import Mesh
from jax.sharding import PartitionSpec as P


PLANE = ("xh", "y")
CHIPS = ("xl", "xh", "y")
HIDPLANE = ("xl", "c", "xh", "y")
BF16 = jnp.bfloat16
F32 = jnp.float32


MOVES = (
    ("z", 8, 1, 1),
    ("z", 8, 2, 1),
    ("z", 8, 4, 1),
    ("y", 4, 1, 1),
    ("y", 4, 2, 1),
    ("xh", 2, 1, 1),
    ("xl", 2, 1, 0),
)


def trade(value, axes):
    return lax.all_to_all(value, axes, 0, 0, tiled=True)


def share(value, axes, count):
    return trade(jnp.broadcast_to(value[None], (count,) + value.shape), axes)


def dot_first(left, right):
    return lax.dot_general(left, right, (((0,), (0,)), ((), ())), preferred_element_type=F32)


def dot_last(left, right):
    return lax.dot_general(left, right, (((1,), (1,)), ((), ())), preferred_element_type=F32)


def pack_kernel(in_hbm, grad_hbm, gate_hbm, up_hbm, down_hbm, out_ref, *scratch):
    in_ref, grad_ref, gate_ref, up_ref, down_ref, held, in_sems, out_sems = scratch
    vals = in_ref.shape[1]
    peers = out_ref.shape[0]
    own = (out_ref.shape[2] - 2 * vals) // 3
    groups = peers // 2
    small = [
        pltpu.make_async_copy(in_hbm, in_ref, in_sems.at[3 * groups]),
        pltpu.make_async_copy(grad_hbm, grad_ref, in_sems.at[3 * groups + 1]),
    ]
    for copy in small:
        copy.start()
    loads = []
    sides = ((gate_hbm, gate_ref), (up_hbm, up_ref), (down_hbm, down_ref))
    for group in range(groups):
        here = pl.ds(group * 2 * own, 2 * own)
        for i, (source, target) in enumerate(sides):
            sem = in_sems.at[3 * group + i]
            loads.append(pltpu.make_async_copy(source.at[:, here], target.at[:, here], sem))
            loads[-1].start()
    for copy in small:
        copy.wait()
    copies = []
    for peer in range(peers):
        if peer % 2 == 0:
            for i in range(3):
                loads[3 * (peer // 2) + i].wait()
        here = slice(peer * own, (peer + 1) * own)
        held[peer, :, :vals] = in_ref[...]
        held[peer, :, vals : 2 * vals] = grad_ref[...]
        start = 2 * vals
        for _, ref in sides:
            held[peer, :, start : start + own] = ref[:, here]
            start += own
        copies.append(pltpu.make_async_copy(held.at[peer], out_ref.at[peer], out_sems.at[peer]))
        copies[-1].start()
    for copy in copies:
        copy.wait()


def pack(inputs_t, out_grad_t, w_gate, w_up, w_down_t, peers):
    feats, vals = inputs_t.shape
    shape = (peers, feats, 2 * vals + 3 * (w_gate.shape[1] // peers))
    arrays = (inputs_t, out_grad_t, w_gate, w_up, w_down_t)
    return pl.pallas_call(
        pack_kernel,
        in_specs=[pl.BlockSpec(memory_space=pl.ANY)] * 5,
        out_specs=pl.BlockSpec(memory_space=pl.ANY),
        out_shape=jax.ShapeDtypeStruct(shape, BF16),
        scratch_shapes=[pltpu.VMEM(value.shape, BF16) for value in arrays]
        + [
            pltpu.VMEM(shape, BF16),
            pltpu.SemaphoreType.DMA((3 * (peers // 2) + 2,)),
            pltpu.SemaphoreType.DMA((peers,)),
        ],
        name="pack",
    )(*arrays)


def fan_kernel(got_ref, out_ref, held, sems):
    n_z, _, wide = got_ref.shape
    feats = 64
    for place in range(wide // feats):
        here = slice(place * feats, (place + 1) * feats)
        for z in range(0, n_z, 2):
            start = (place * n_z + z) * feats
            pair = jnp.concatenate([got_ref[z, :, here], got_ref[z + 1, :, here]], axis=1)
            held[:, start : start + 2 * feats] = pair
    copies = [
        pltpu.make_async_copy(held, out_ref.at[i], sems.at[i]) for i in range(out_ref.shape[0])
    ]
    for copy in copies:
        copy.start()
    for copy in copies:
        copy.wait()


def fan_out(got, count):
    n_z, rows, wide = got.shape
    return pl.pallas_call(
        fan_kernel,
        in_specs=[pl.BlockSpec(memory_space=pltpu.VMEM)],
        out_specs=pl.BlockSpec(memory_space=pl.ANY),
        out_shape=jax.ShapeDtypeStruct((count, rows, n_z * wide), BF16),
        scratch_shapes=[pltpu.VMEM((rows, n_z * wide), BF16), pltpu.SemaphoreType.DMA((count,))],
        compiler_params=pltpu.CompilerParams(vmem_limit_bytes=4 * 1024 * 1024),
        name="fan_out",
    )(got)


def backward_kernel(first, grads_ref, got_ref, out_ref):
    weights = got_ref[:, first : first + grads_ref.shape[1]]
    out_ref[...] = dot_last(grads_ref[...], weights).astype(out_ref.dtype)


def backward(first, grads, got):
    vmem = pl.BlockSpec(memory_space=pltpu.VMEM)
    return pl.pallas_call(
        functools.partial(backward_kernel, first),
        out_shape=jax.ShapeDtypeStruct((grads.shape[0], got.shape[0]), BF16),
        in_specs=[vmem] * 2,
        compiler_params=pltpu.CompilerParams(vmem_limit_bytes=8 * 1024 * 1024),
        name="backward",
    )(grads, got)


def gram_kernel(train_ref, val_ref, out_ref):
    out_ref[...] = dot_last(val_ref[...], train_ref[...])


def gram(train, val):
    tokens, width = train.shape
    rows = val.shape[0]
    block = 128
    return pl.pallas_call(
        gram_kernel,
        grid=(tokens // block,),
        in_specs=[
            pl.BlockSpec((block, width), lambda i: (i, 0)),
            pl.BlockSpec((rows, width), lambda i: (0, 0)),
        ],
        out_specs=pl.BlockSpec((rows, block), lambda i: (0, i)),
        out_shape=jax.ShapeDtypeStruct((rows, tokens), F32),
        compiler_params=pltpu.CompilerParams(vmem_limit_bytes=10 * 1024 * 1024),
        name="gram",
    )(train, val)


def block_kernel(own_ref, block_ref):
    rows, feats = block_ref.shape
    tile = (lax.axis_index("xh") * 4 + lax.axis_index("y")) * 8 + lax.axis_index("z")
    row = pl.multiple_of(lax.axis_index("xl") * rows, rows)
    col = pl.multiple_of((tile // 2) * (2 * feats), 2 * feats)
    found = own_ref[pl.ds(row, rows), pl.ds(col, 2 * feats)].astype(F32)
    half = jnp.where(tile % 2 == 0, found[:, :feats], found[:, feats:])
    block_ref[...] = half.astype(BF16)


def pair_kernel(scale, train_ref, own_ref, other_ref, gram_own_ref, gram_other_ref, out_ref):
    val = jnp.concatenate([own_ref[...], other_ref[...]], axis=0)
    grad_gram = dot_last(val, train_ref[...])
    count = own_ref.shape[0]
    total = gram_own_ref[...] * grad_gram[:count] + gram_other_ref[...] * grad_gram[count:]
    total = jnp.sum(total, axis=0, keepdims=True) * scale
    out_ref[...] = total.reshape(out_ref.shape)


VMEM = pl.BlockSpec(memory_space=pltpu.VMEM)
COVER = pl.CostEstimate(flops=10**10, bytes_accessed=32 * 2**20, transcendentals=0)


def own_block(own, rows, feats):
    return pl.pallas_call(
        block_kernel,
        out_shape=jax.ShapeDtypeStruct((rows, feats), BF16),
        in_specs=[VMEM],
        out_specs=VMEM,
        compiler_params=pltpu.CompilerParams(vmem_limit_bytes=8 * 1024 * 1024),
        cost_estimate=COVER,
        name="own_block",
    )(own)


def pair_values(scale, train, own, other, gram_own, gram_other):
    return pl.pallas_call(
        functools.partial(pair_kernel, scale),
        out_shape=jax.ShapeDtypeStruct((train.shape[0],), F32),
        in_specs=[VMEM] * 5,
        out_specs=VMEM,
        compiler_params=pltpu.CompilerParams(vmem_limit_bytes=24 * 1024 * 1024),
        name="pair_values",
    )(train, own, other, gram_own, gram_other)


def act_grads(gate_pre, up_pre, hid_grad):
    logistic = jax.nn.sigmoid(gate_pre)
    grad_gate = (hid_grad * up_pre * logistic * (1.0 + gate_pre * (1.0 - logistic))).astype(BF16)
    grad_up = (hid_grad * gate_pre * logistic).astype(BF16)
    return jnp.concatenate([grad_gate, grad_up], axis=1)


def local(
    val_inputs, val_out_grad, w_gate, w_up, w_down, val_attn_inputs, train_inputs, train_grads
):
    feats, units = w_gate.shape
    vals = val_inputs.shape[0]
    n_plane = lax.axis_size(PLANE)
    n_z = lax.axis_size("z")
    n_chips = lax.axis_size(CHIPS)
    n_hidplane = lax.axis_size(HIDPLANE)
    own = units // n_plane
    wide = feats * n_plane

    width = train_inputs.shape[1]
    attn_rows = val_attn_inputs.shape[0]
    chunk = vals // n_hidplane
    rows_z = vals // n_z
    swap = [(0, 1), (1, 0)]
    first_w, first_down = 2 * vals, 2 * vals + 2 * own

    row = lax.axis_index(HIDPLANE) * chunk
    attn = val_attn_inputs
    for axis, count, bit, dim in MOVES:
        pairs = [(i, i ^ bit) for i in range(count)]
        theirs = lax.ppermute(attn, axis, pairs)
        high = (lax.axis_index(axis) & bit) != 0
        attn = jnp.concatenate(
            [jnp.where(high, theirs, attn), jnp.where(high, attn, theirs)], axis=dim
        )
    sent = pack(val_inputs.T, val_out_grad.T, w_gate, w_up, w_down.T, n_plane)
    got = trade(sent, PLANE).reshape(wide, 3 * own + 2 * vals)
    back_w = got[:, first_w:first_down]
    partial = jnp.concatenate(
        [dot_first(got[:, :vals], back_w), dot_first(got[:, vals:first_w], got[:, first_down:])],
        axis=1,
    ).astype(BF16)
    parts = trade(partial.reshape(n_z, rows_z, 3 * own), "z")
    pre = jnp.sum(parts.astype(F32), axis=0)
    grads = act_grads(pre[:, :own], pre[:, own : 2 * own], pre[:, 2 * own :])
    grads = share(grads, "z", n_z).reshape(vals, 2 * own)
    attn_other = lax.ppermute(attn, "c", swap)
    part = backward(first_w, grads, got)
    parts = trade(part.reshape(n_hidplane, chunk, wide), HIDPLANE)

    gram_own = gram(train_inputs, attn)
    gram_other = gram(train_inputs, attn_other)
    dx = jnp.sum(parts.astype(F32), axis=0)
    mine = lax.dynamic_slice_in_dim(got[:, vals:first_w], row, chunk, 1).T
    mine = lax.optimization_barrier(mine)
    val_grad = (mine.astype(F32) + dx).astype(BF16)
    val_z = share(val_grad, "z", n_z)
    sent = fan_out(val_z, n_chips)
    val_own = trade(sent, CHIPS).reshape(n_chips * chunk, width)
    val_other = lax.ppermute(val_own, "c", swap)
    block = own_block(val_own, attn_rows, feats)
    scale = 1.0 / (width * math.sqrt(vals))
    influence = pair_values(scale, train_grads, val_own, val_other, gram_own, gram_other)
    return (influence, block)


def solution(mesh):
    fine = Mesh(mesh.devices.reshape(2, 2, 2, 4, 8), ("xl", "c", "xh", "y", "z"))
    tok = ("xh", "y", "z")
    hid = ("xl", "c")
    placed = (
        P(None, tok),
        P(None, tok),
        P(tok, hid),
        P(tok, hid),
        P(hid, tok),
        P(hid, tok),
        P(hid + tok, None),
        P(hid + tok, None),
    )
    return jax.shard_map(
        local,
        mesh=fine,
        in_specs=placed,
        out_specs=(P(hid + tok), P(hid, tok)),
        check_vma=False,
    )
```

```python
import functools
import math

import jax
import jax.numpy as jnp
from jax import lax
from jax.experimental import pallas as pl
from jax.experimental.pallas import tpu as pltpu
from jax.sharding import Mesh
from jax.sharding import PartitionSpec as P


PLANE = ("xh", "y")
CHIPS = ("xl", "xh", "y")
HIDPLANE = ("xl", "c", "xh", "y")
BF16 = jnp.bfloat16
F32 = jnp.float32


MOVES = (
    ("z", 8, 1, 1),
    ("z", 8, 2, 1),
    ("z", 8, 4, 1),
    ("y", 4, 1, 1),
    ("y", 4, 2, 1),
    ("xh", 2, 1, 1),
    ("xl", 2, 1, 0),
)


def trade(value, axes):
    return lax.all_to_all(value, axes, 0, 0, tiled=True)


def share(value, axes, count):
    return trade(jnp.broadcast_to(value[None], (count,) + value.shape), axes)


def dot_first(left, right):
    return lax.dot_general(left, right, (((0,), (0,)), ((), ())), preferred_element_type=F32)


def dot_last(left, right):
    return lax.dot_general(left, right, (((1,), (1,)), ((), ())), preferred_element_type=F32)


def pack_kernel(in_hbm, grad_hbm, gate_hbm, up_hbm, down_hbm, out_ref, *scratch):
    in_ref, grad_ref, gate_ref, up_ref, down_ref, held, in_sems, out_sems = scratch
    vals = in_ref.shape[1]
    peers = out_ref.shape[0]
    own = (out_ref.shape[2] - 2 * vals) // 3
    groups = peers // 2
    small = [
        pltpu.make_async_copy(in_hbm, in_ref, in_sems.at[3 * groups]),
        pltpu.make_async_copy(grad_hbm, grad_ref, in_sems.at[3 * groups + 1]),
    ]
    for copy in small:
        copy.start()
    loads = []
    sides = ((gate_hbm, gate_ref), (up_hbm, up_ref), (down_hbm, down_ref))
    for group in range(groups):
        here = pl.ds(group * 2 * own, 2 * own)
        for i, (source, target) in enumerate(sides):
            sem = in_sems.at[3 * group + i]
            loads.append(pltpu.make_async_copy(source.at[:, here], target.at[:, here], sem))
            loads[-1].start()
    for copy in small:
        copy.wait()
    copies = []
    for peer in range(peers):
        if peer % 2 == 0:
            for i in range(3):
                loads[3 * (peer // 2) + i].wait()
        here = slice(peer * own, (peer + 1) * own)
        held[peer, :, :vals] = in_ref[...]
        held[peer, :, vals : 2 * vals] = grad_ref[...]
        start = 2 * vals
        for _, ref in sides:
            held[peer, :, start : start + own] = ref[:, here]
            start += own
        copies.append(pltpu.make_async_copy(held.at[peer], out_ref.at[peer], out_sems.at[peer]))
        copies[-1].start()
    for copy in copies:
        copy.wait()


def pack(inputs_t, out_grad_t, w_gate, w_up, w_down_t, peers):
    feats, vals = inputs_t.shape
    shape = (peers, feats, 2 * vals + 3 * (w_gate.shape[1] // peers))
    arrays = (inputs_t, out_grad_t, w_gate, w_up, w_down_t)
    return pl.pallas_call(
        pack_kernel,
        in_specs=[pl.BlockSpec(memory_space=pl.ANY)] * 5,
        out_specs=pl.BlockSpec(memory_space=pl.ANY),
        out_shape=jax.ShapeDtypeStruct(shape, BF16),
        scratch_shapes=[pltpu.VMEM(value.shape, BF16) for value in arrays]
        + [
            pltpu.VMEM(shape, BF16),
            pltpu.SemaphoreType.DMA((3 * (peers // 2) + 2,)),
            pltpu.SemaphoreType.DMA((peers,)),
        ],
        name="pack",
    )(*arrays)


def fan_kernel(got_ref, out_ref, held, sems):
    n_z, _, wide = got_ref.shape
    feats = 64
    for place in range(wide // feats):
        here = slice(place * feats, (place + 1) * feats)
        for z in range(0, n_z, 2):
            start = (place * n_z + z) * feats
            pair = jnp.concatenate([got_ref[z, :, here], got_ref[z + 1, :, here]], axis=1)
            held[:, start : start + 2 * feats] = pair
    copies = [
        pltpu.make_async_copy(held, out_ref.at[i], sems.at[i]) for i in range(out_ref.shape[0])
    ]
    for copy in copies:
        copy.start()
    for copy in copies:
        copy.wait()


def fan_out(got, count):
    n_z, rows, wide = got.shape
    return pl.pallas_call(
        fan_kernel,
        in_specs=[pl.BlockSpec(memory_space=pltpu.VMEM)],
        out_specs=pl.BlockSpec(memory_space=pl.ANY),
        out_shape=jax.ShapeDtypeStruct((count, rows, n_z * wide), BF16),
        scratch_shapes=[pltpu.VMEM((rows, n_z * wide), BF16), pltpu.SemaphoreType.DMA((count,))],
        compiler_params=pltpu.CompilerParams(vmem_limit_bytes=4 * 1024 * 1024),
        name="fan_out",
    )(got)


def backward_kernel(first, grads_ref, got_ref, out_ref):
    weights = got_ref[:, first : first + grads_ref.shape[1]]
    out_ref[...] = dot_last(grads_ref[...], weights).astype(out_ref.dtype)


def backward(first, grads, got):
    vmem = pl.BlockSpec(memory_space=pltpu.VMEM)
    return pl.pallas_call(
        functools.partial(backward_kernel, first),
        out_shape=jax.ShapeDtypeStruct((grads.shape[0], got.shape[0]), BF16),
        in_specs=[vmem] * 2,
        compiler_params=pltpu.CompilerParams(vmem_limit_bytes=8 * 1024 * 1024),
        name="backward",
    )(grads, got)


def gram_kernel(train_ref, val_ref, out_ref):
    out_ref[...] = dot_last(val_ref[...], train_ref[...])


def gram(train, val):
    tokens, width = train.shape
    rows = val.shape[0]
    block = 128
    return pl.pallas_call(
        gram_kernel,
        grid=(tokens // block,),
        in_specs=[
            pl.BlockSpec((block, width), lambda i: (i, 0)),
            pl.BlockSpec((rows, width), lambda i: (0, 0)),
        ],
        out_specs=pl.BlockSpec((rows, block), lambda i: (0, i)),
        out_shape=jax.ShapeDtypeStruct((rows, tokens), F32),
        compiler_params=pltpu.CompilerParams(vmem_limit_bytes=10 * 1024 * 1024),
        name="gram",
    )(train, val)


def block_kernel(own_ref, block_ref):
    rows, feats = block_ref.shape
    tile = (lax.axis_index("xh") * 4 + lax.axis_index("y")) * 8 + lax.axis_index("z")
    row = pl.multiple_of(lax.axis_index("xl") * rows, rows)
    col = pl.multiple_of((tile // 2) * (2 * feats), 2 * feats)
    found = own_ref[pl.ds(row, rows), pl.ds(col, 2 * feats)].astype(F32)
    half = jnp.where(tile % 2 == 0, found[:, :feats], found[:, feats:])
    block_ref[...] = half.astype(BF16)


def pair_kernel(scale, train_ref, own_ref, other_ref, gram_own_ref, gram_other_ref, out_ref):
    val = jnp.concatenate([own_ref[...], other_ref[...]], axis=0)
    grad_gram = dot_last(val, train_ref[...])
    count = own_ref.shape[0]
    total = gram_own_ref[...] * grad_gram[:count] + gram_other_ref[...] * grad_gram[count:]
    total = jnp.sum(total, axis=0, keepdims=True) * scale
    out_ref[...] = total.reshape(out_ref.shape)


VMEM = pl.BlockSpec(memory_space=pltpu.VMEM)
COVER = pl.CostEstimate(flops=10**10, bytes_accessed=32 * 2**20, transcendentals=0)


def own_block(own, rows, feats):
    return pl.pallas_call(
        block_kernel,
        out_shape=jax.ShapeDtypeStruct((rows, feats), BF16),
        in_specs=[VMEM],
        out_specs=VMEM,
        compiler_params=pltpu.CompilerParams(vmem_limit_bytes=8 * 1024 * 1024),
        cost_estimate=COVER,
        name="own_block",
    )(own)


def pair_values(scale, train, own, other, gram_own, gram_other):
    return pl.pallas_call(
        functools.partial(pair_kernel, scale),
        out_shape=jax.ShapeDtypeStruct((train.shape[0],), F32),
        in_specs=[VMEM] * 5,
        out_specs=VMEM,
        compiler_params=pltpu.CompilerParams(vmem_limit_bytes=24 * 1024 * 1024),
        name="pair_values",
    )(train, own, other, gram_own, gram_other)


def act_grads(gate_pre, up_pre, hid_grad):
    logistic = jax.nn.sigmoid(gate_pre)
    grad_gate = (hid_grad * up_pre * logistic * (1.0 + gate_pre * (1.0 - logistic))).astype(BF16)
    grad_up = (hid_grad * gate_pre * logistic).astype(BF16)
    return jnp.concatenate([grad_gate, grad_up], axis=1)


def act_kernel(parts_ref, out_ref, held, sems):
    pre = jnp.sum(parts_ref[...].astype(F32), axis=0)
    own = pre.shape[1] // 3
    held[...] = act_grads(pre[:, :own], pre[:, own : 2 * own], pre[:, 2 * own :])
    copies = [
        pltpu.make_async_copy(held, out_ref.at[i], sems.at[i]) for i in range(out_ref.shape[0])
    ]
    for copy in copies:
        copy.start()
    for copy in copies:
        copy.wait()


def act_slots(parts):
    count, rows, wide = parts.shape
    kept = 2 * wide // 3
    return pl.pallas_call(
        act_kernel,
        in_specs=[pl.BlockSpec(memory_space=pltpu.VMEM)],
        out_specs=pl.BlockSpec(memory_space=pl.ANY),
        out_shape=jax.ShapeDtypeStruct((count, rows, kept), BF16),
        scratch_shapes=[pltpu.VMEM((rows, kept), BF16), pltpu.SemaphoreType.DMA((count,))],
        compiler_params=pltpu.CompilerParams(vmem_limit_bytes=4 * 1024 * 1024),
        name="act_slots",
    )(parts)


def local(
    val_inputs, val_out_grad, w_gate, w_up, w_down, val_attn_inputs, train_inputs, train_grads
):
    feats, units = w_gate.shape
    vals = val_inputs.shape[0]
    n_plane = lax.axis_size(PLANE)
    n_z = lax.axis_size("z")
    n_chips = lax.axis_size(CHIPS)
    n_hidplane = lax.axis_size(HIDPLANE)
    own = units // n_plane
    wide = feats * n_plane

    width = train_inputs.shape[1]
    attn_rows = val_attn_inputs.shape[0]
    chunk = vals // n_hidplane
    rows_z = vals // n_z
    swap = [(0, 1), (1, 0)]
    first_w, first_down = 2 * vals, 2 * vals + 2 * own

    row = lax.axis_index(HIDPLANE) * chunk
    attn = val_attn_inputs
    for axis, count, bit, dim in MOVES:
        pairs = [(i, i ^ bit) for i in range(count)]
        theirs = lax.ppermute(attn, axis, pairs)
        high = (lax.axis_index(axis) & bit) != 0
        attn = jnp.concatenate(
            [jnp.where(high, theirs, attn), jnp.where(high, attn, theirs)], axis=dim
        )
    sent = pack(val_inputs.T, val_out_grad.T, w_gate, w_up, w_down.T, n_plane)
    got = trade(sent, PLANE).reshape(wide, 3 * own + 2 * vals)
    back_w = got[:, first_w:first_down]
    partial = jnp.concatenate(
        [dot_first(got[:, :vals], back_w), dot_first(got[:, vals:first_w], got[:, first_down:])],
        axis=1,
    ).astype(BF16)
    parts = trade(partial.reshape(n_z, rows_z, 3 * own), "z")
    sent = act_slots(parts)
    grads = trade(sent, "z").reshape(vals, 2 * own)
    attn_other = lax.ppermute(attn, "c", swap)
    part = backward(first_w, grads, got)
    parts = trade(part.reshape(n_hidplane, chunk, wide), HIDPLANE)

    gram_own = gram(train_inputs, attn)
    gram_other = gram(train_inputs, attn_other)
    dx = jnp.sum(parts.astype(F32), axis=0)
    mine = lax.dynamic_slice_in_dim(got[:, vals:first_w], row, chunk, 1).T
    mine = lax.optimization_barrier(mine)
    val_grad = (mine.astype(F32) + dx).astype(BF16)
    val_z = share(val_grad, "z", n_z)
    sent = fan_out(val_z, n_chips)
    val_own = trade(sent, CHIPS).reshape(n_chips * chunk, width)
    val_other = lax.ppermute(val_own, "c", swap)
    block = own_block(val_own, attn_rows, feats)
    scale = 1.0 / (width * math.sqrt(vals))
    influence = pair_values(scale, train_grads, val_own, val_other, gram_own, gram_other)
    return (influence, block)


def solution(mesh):
    fine = Mesh(mesh.devices.reshape(2, 2, 2, 4, 8), ("xl", "c", "xh", "y", "z"))
    tok = ("xh", "y", "z")
    hid = ("xl", "c")
    placed = (
        P(None, tok),
        P(None, tok),
        P(tok, hid),
        P(tok, hid),
        P(hid, tok),
        P(hid, tok),
        P(hid + tok, None),
        P(hid + tok, None),
    )
    return jax.shard_map(
        local,
        mesh=fine,
        in_specs=placed,
        out_specs=(P(hid + tok), P(hid, tok)),
        check_vma=False,
    )
```
